256 devices in a mesh: hi: 32 (over x, y, core), lo: 8 (over z).
Axes of the slice: x: 4, y: 4, z: 8, core: 2. Of those that a mesh axis runs over, the one named last changes fastest.
Arguments:
- embeddings: bfloat16 [131072, 256], P(('hi', 'lo')), may hold values from -6 to 6
- leaf_order: int32 [512, 256], P(('hi', 'lo')), may hold values from 0 to 255, as said below
- vectors_now: float32 [131072, 128], P(('hi', 'lo')), may hold values from -45 to 45
- vectors_prior: float32 [131072, 128], P(('hi', 'lo')), may hold values from -6 to 6
- leaf_bases: float32 [131072, 128], P(('hi', 'lo')), may hold values from -0.375 to 0.375
- low_transfer: bfloat16 [768, 128, 128], P(('hi', 'lo')), may hold values from -0.4375 to 0.4375
- low_couple: bfloat16 [768, 128, 128], P(('hi', 'lo')), may hold values from -0.18 to 0.18, as said below
- middle_transfer: bfloat16 [32, 6, 128, 128], P('hi'), may hold values from -0.4375 to 0.4375
- middle_couple: bfloat16 [32, 6, 128, 128], P('hi'), may hold values from -0.18 to 0.18, as said below
- top_transfer: bfloat16 [60, 128, 128], replicated, may hold values from -0.4375 to 0.4375
- top_couple: bfloat16 [62, 128, 128], replicated, may hold values from -0.18 to 0.18, as said below
Outputs:
- filtered: float32 [131072, 128], P(('hi', 'lo'))
- filtered_prior: float32 [131072, 128], P(('hi', 'lo'))
- gram_matrix: float32 [128, 128], replicated
The draws below stay inside these ranges and needn't reach their ends.
Inputs may be any that keep to these rules, and one draw needn't show every extreme that they name: `leaf_order`: the 256 entries of each leaf are a permutation of 0 to 255. `low_couple`: the matrix of each node is the transpose of its sibling's matrix. `middle_couple`: the matrix of each node is the transpose of its sibling's matrix. `top_couple`: the matrix of each node is the transpose of its sibling's matrix.
All inputs are finite; a program needn't handle non-finite values.
Results may differ from the reference program's by a relative error of at most 0.0003.
Values sent between devices are 32-bit elements; how exact they have to be, the bound alone decides.
No kernel may reach another device: no remote copies, remote signals or barrier semaphores. Data moves between devices by JAX's collectives and lax.ppermute only.
A program may use at most 128 MiB of HBM per device.

```python
import jax
import jax.numpy as jnp
import numpy as np
from jax import lax

EMB = 256
LEAF = 256
RANK = 128
VECS = 128
DEGREE = 6
LEAF_DEV = 2
LEAVES = 512
POINTS = 131072
HI_LEVELS = 5
LO_LEVELS = 3
DEV_LEVELS = 1
TOP_NODES = 62
TOP_TRANSFERS = 60
MIDDLE_NODES = 6
LOW_NODES = 768
N_HI = 32
N_LO = 8


COUPLE_SCALE = 0.4


COUPLE_BOUND = 0.18


def couple_base(key, shape):
    values = jax.random.normal(key, shape, jnp.float32)
    return jnp.clip(values * (COUPLE_SCALE / RANK ** 0.5), -COUPLE_BOUND, COUPLE_BOUND)


def paired(values, partner, leftward):
    mirrored = jnp.swapaxes(values[partner], 1, 2)
    return jnp.where(jnp.asarray(leftward)[:, None, None], values, mirrored)


def draw_top_couple(key, part):
    positions = np.arange(TOP_NODES)
    return paired(couple_base(key, (TOP_NODES, RANK, RANK)), positions ^ 1, positions % 2 == 0).astype(jnp.bfloat16)


def draw_middle_couple(key, part):
    total = N_HI * MIDDLE_NODES
    indices = np.arange(total)
    within = indices % MIDDLE_NODES
    partner = indices - within + (within ^ 1)
    values = paired(couple_base(key, (total, RANK, RANK)), partner, within % 2 == 0)
    return values.reshape(N_HI, MIDDLE_NODES, RANK, RANK).astype(jnp.bfloat16)


def draw_low_couple(key, part):
    stride = 2 * LEAF_DEV - 1
    indices = np.arange(LOW_NODES)
    device = indices // stride
    within = indices % stride
    partner = np.where(within == 0, (device ^ 1) * stride, np.where(within % 2 == 1, indices + 1, indices - 1))
    leftward = np.where(within == 0, device % 2 == 0, within % 2 == 1)
    return paired(couple_base(key, (LOW_NODES, RANK, RANK)), partner, leftward).astype(jnp.bfloat16)


def draw_leaf_order(key, part):
    subkeys = jax.random.split(key, LEAVES)
    return jax.vmap(lambda single_key: jax.random.permutation(single_key, LEAF))(subkeys).astype(jnp.int32)


def draw_vectors_now(key, part):
    subkeys = jax.random.split(key, 3)
    position_share = jnp.arange(POINTS, dtype=jnp.float32) / POINTS
    rising = 3.0 ** (position_share - 0.5)
    row_spread = 10.0 ** (jax.random.uniform(subkeys[0], (POINTS,), jnp.float32) - 0.5)
    column_spread = 10.0 ** (jax.random.uniform(subkeys[1], (VECS,), jnp.float32) - 0.5)
    scales = (rising * row_spread)[:, None] * column_spread[None, :]
    random_part = jnp.clip(jax.random.normal(subkeys[2], (POINTS, VECS), jnp.float32), -5.0, 5.0)
    return 0.5 * random_part * scales


def block_levels(stream_key, shape, cuts, low, high):
    factor_of, own = 1.0, jax.random.fold_in(stream_key, 6)
    for dim, shards_of in cuts:
        draws = jnp.exp(jax.random.uniform(jax.random.fold_in(own, dim), (shards_of,), jnp.float32, low / len(cuts), high / len(cuts)))
        factor_of = factor_of * jnp.repeat(draws, shape[dim] // shards_of).reshape([-1 if axis == dim else 1 for axis in range(len(shape))])
    return factor_of


def scatter_about(stream_key, extent, width, most, cuts=(), kind=jnp.bfloat16):
    drawn = jax.random.normal(stream_key, extent, jnp.float32) * width
    if len(cuts) > 0:
        drawn = block_levels(stream_key, extent, cuts, -0.22, 0.18) * drawn
    return jnp.clip(drawn, min=-most, max=most).astype(kind)


def setup_inputs(seed: int = 0) -> dict:
    key_of = jax.random.split(jax.random.key(seed), 12)
    embeddings = scatter_about(key_of[0], (POINTS, EMB), 1.0, 6.0, ((0, 256),))
    leaf_order = draw_leaf_order(jax.random.fold_in(key_of[11], 71), 0)
    vectors_now = draw_vectors_now(jax.random.fold_in(key_of[11], 71), 0)
    vectors_prior = scatter_about(key_of[3], (POINTS, VECS), 1.0, 6.0, ((0, 256),), jnp.float32)
    leaf_bases = scatter_about(key_of[4], (POINTS, RANK), LEAF ** -0.5, 0.375, ((0, 256),), jnp.float32)
    low_transfer = scatter_about(key_of[5], (LOW_NODES, RANK, RANK), (RANK * 1414 // 1000) ** -0.5, 0.4375, ((0, 256),))
    low_couple = draw_low_couple(jax.random.fold_in(key_of[11], 71), 0)
    middle_transfer = scatter_about(key_of[7], (N_HI, MIDDLE_NODES, RANK, RANK), (RANK * 1414 // 1000) ** -0.5, 0.4375, ((0, 32),))
    middle_couple = draw_middle_couple(jax.random.fold_in(key_of[11], 71), 0)
    top_transfer = scatter_about(key_of[9], (TOP_TRANSFERS, RANK, RANK), (RANK * 1414 // 1000) ** -0.5, 0.4375)
    top_couple = draw_top_couple(jax.random.fold_in(key_of[11], 71), 0)
    return dict(embeddings=embeddings, leaf_order=leaf_order, vectors_now=vectors_now, vectors_prior=vectors_prior, leaf_bases=leaf_bases, low_transfer=low_transfer, low_couple=low_couple, middle_transfer=middle_transfer, middle_couple=middle_couple, top_transfer=top_transfer, top_couple=top_couple)


KERNEL_WIDTH = 0.5
FILTER_CENTER = 2.0
FILTER_HALF = 10.0
PRECISE = lax.Precision.HIGHEST


def flip_pairs(values):
    shaped = values.reshape((values.shape[0] // 2, 2) + values.shape[1:])
    return shaped[:, ::-1].reshape(values.shape)


def kernel_blocks(tree_points):
    widened = tree_points.astype(jnp.float32)
    inner_products = jnp.einsum("npe,nqe->npq", widened, widened, precision=PRECISE)
    squares = jnp.diagonal(inner_products, axis1=1, axis2=2)
    distance = squares[:, :, None] + squares[:, None, :] - 2.0 * inner_products
    return jnp.exp(-distance / (KERNEL_WIDTH * EMB))


def level_tables(low_transfer, low_couple, middle_transfer, middle_couple, top_transfer, top_couple):
    transfers = []
    couples = []
    for tree_depth in range(1, HI_LEVELS + 1):
        number = 2 ** tree_depth
        couples.append(top_couple[number - 2:2 * number - 2].astype(jnp.float32))
        if tree_depth >= 2:
            transfers.append(top_transfer[number - 4:2 * number - 4].astype(jnp.float32))
        else:
            transfers.append(None)
    for tree_depth in range(1, LO_LEVELS):
        number = 2 ** tree_depth
        transfers.append(middle_transfer[:, number - 2:2 * number - 2].reshape(N_HI * number, RANK, RANK).astype(jnp.float32))
        couples.append(middle_couple[:, number - 2:2 * number - 2].reshape(N_HI * number, RANK, RANK).astype(jnp.float32))
    low_shaped = low_transfer.reshape(N_HI * N_LO, 2 * LEAF_DEV - 1, RANK, RANK)
    couple_shaped = low_couple.reshape(N_HI * N_LO, 2 * LEAF_DEV - 1, RANK, RANK)
    for tree_depth in range(0, DEV_LEVELS + 1):
        number = 2 ** tree_depth
        transfers.append(low_shaped[:, number - 1:2 * number - 1].reshape(N_HI * N_LO * number, RANK, RANK).astype(jnp.float32))
        couples.append(couple_shaped[:, number - 1:2 * number - 1].reshape(N_HI * N_LO * number, RANK, RANK).astype(jnp.float32))
    return transfers, couples


def apply_kernel(current, blocks, basis_rows, transfers, couples):
    levels = len(couples)
    coeffs = [None] * levels
    coupled = [None] * levels
    coeffs[levels - 1] = jnp.einsum("npr,npv->nrv", basis_rows, current, precision=PRECISE)
    for position in range(levels - 1, -1, -1):
        coupled[position] = jnp.einsum("nrs,nsv->nrv", couples[position], flip_pairs(coeffs[position]), precision=PRECISE)
        if position >= 1:
            lifted = jnp.einsum("nrs,nrv->nsv", transfers[position], coeffs[position], precision=PRECISE)
            coeffs[position - 1] = lifted[0::2] + lifted[1::2]
    downward = coupled[0]
    for position in range(1, levels):
        downward = coupled[position] + jnp.einsum("nrs,nsv->nrv", transfers[position], jnp.repeat(downward, 2, axis=0), precision=PRECISE)
    nearby = jnp.einsum("npq,nqv->npv", blocks, current, precision=PRECISE)
    return nearby + jnp.einsum("npr,nrv->npv", basis_rows, downward, precision=PRECISE)


def reference(embeddings, leaf_order, vectors_now, vectors_prior, leaf_bases, low_transfer, low_couple, middle_transfer, middle_couple, top_transfer, top_couple):
    ordering = leaf_order[:, :, None]

    def tree_order(values):
        return jnp.take_along_axis(values.reshape(LEAVES, LEAF, values.shape[-1]), ordering, axis=1)

    blocks = kernel_blocks(tree_order(embeddings))
    basis_rows = leaf_bases.reshape(LEAVES, LEAF, RANK)
    transfers, couples = level_tables(low_transfer, low_couple, middle_transfer, middle_couple, top_transfer, top_couple)
    previous = tree_order(vectors_prior)
    current = tree_order(vectors_now)
    for degree_index in range(DEGREE):
        applied = apply_kernel(current, blocks, basis_rows, transfers, couples)
        previous, current = current, (2.0 / FILTER_HALF) * (applied - FILTER_CENTER * current) - previous
    flattened = current.reshape(POINTS, VECS)
    gram_matrix = jnp.dot(flattened.T, flattened, precision=PRECISE) / POINTS
    inverse = jnp.argsort(leaf_order, axis=1)[:, :, None]
    filtered = jnp.take_along_axis(current, inverse, axis=1).reshape(POINTS, VECS)
    filtered_prior = jnp.take_along_axis(previous, inverse, axis=1).reshape(POINTS, VECS)
    return filtered, filtered_prior, gram_matrix
```

```python
import jax
import jax.numpy as jnp
from jax import lax
from jax.sharding import PartitionSpec as P

DEGREE = 6


KERNEL_WIDTH = 0.5
FILTER_CENTER = 2.0
FILTER_HALF = 10.0
PRECISE = lax.Precision.HIGHEST


def swapped(array, axis, bit):
    return lax.ppermute(array, axis, [(i, i ^ 1 << bit) for i in range(lax.axis_size(axis))])


def flip_pairs(values):
    shaped = values.reshape((values.shape[0] // 2, 2) + values.shape[1:])
    return shaped[:, ::-1].reshape(values.shape)


def select_row(source, position):
    return lax.dynamic_index_in_dim(source, position, 0, keepdims=False).astype(jnp.float32)


def lift_coeffs(transfer, coeffs):
    return jnp.dot(transfer.T, coeffs, precision=PRECISE)


def lift_level(transfer, coeffs):
    lifted = jnp.einsum("nrs,nrv->nsv", transfer, coeffs, precision=PRECISE)
    return lifted[0::2] + lifted[1::2]


def apply_kernel(current, blocks, basis_rows, tables):
    low_transfer, low_couple, middle_transfer, middle_couple, top_transfer, top_couple = tables
    upper_bits = lax.axis_size("hi").bit_length() - 1
    lower_bits = lax.axis_size("lo").bit_length() - 1
    upper_index = lax.axis_index("hi")
    lower_index = lax.axis_index("lo")
    local_bits = current.shape[0].bit_length() - 1
    coeffs = jnp.einsum("npr,npv->nrv", basis_rows, current, precision=PRECISE)
    local_terms = {}
    for tree_depth in range(local_bits, 0, -1):
        offset = 2**tree_depth - 1
        number = 2**tree_depth
        transfer = low_transfer[offset : offset + number].astype(jnp.float32)
        couple = low_couple[offset : offset + number].astype(jnp.float32)
        local_terms[tree_depth] = jnp.einsum(
            "nrs,nsv->nrv", couple, flip_pairs(coeffs), precision=PRECISE
        )
        coeffs = lift_level(transfer, coeffs)
    cluster = coeffs[0]
    descent = []
    for which_bit in range(lower_bits):
        if which_bit == 0:
            transfer = low_transfer[0].astype(jnp.float32)
            couple = low_couple[0].astype(jnp.float32)
        else:
            position = 2 ** (lower_bits - which_bit) - 2 + (lower_index >> which_bit)
            transfer = select_row(middle_transfer[0], position)
            couple = select_row(middle_couple[0], position)
        lifted = lift_coeffs(transfer, cluster)
        partner = swapped(jnp.stack((cluster, lifted)), "lo", which_bit)
        descent.append((jnp.dot(couple, partner[0], precision=PRECISE), transfer))
        cluster = lifted + partner[1]
    for which_bit in range(upper_bits - 1):
        tree_depth = upper_bits - which_bit
        slot_index = upper_index >> which_bit
        transfer = select_row(top_transfer, 2**tree_depth - 4 + slot_index)
        couple = select_row(top_couple, 2**tree_depth - 2 + slot_index)
        lifted = lift_coeffs(transfer, cluster)
        partner = swapped(jnp.stack((cluster, lifted)), "hi", which_bit)
        descent.append((jnp.dot(couple, partner[0], precision=PRECISE), transfer))
        cluster = lifted + partner[1]
    sibling = swapped(cluster, "hi", upper_bits - 1)
    downward = jnp.dot(
        select_row(top_couple, upper_index >> upper_bits - 1), sibling, precision=PRECISE
    )
    for coupled, transfer in reversed(descent):
        downward = coupled + jnp.dot(transfer, downward, precision=PRECISE)
    downward = downward[None]
    for tree_depth in range(1, local_bits + 1):
        offset = 2**tree_depth - 1
        number = 2**tree_depth
        transfer = low_transfer[offset : offset + number].astype(jnp.float32)
        downward = local_terms[tree_depth] + jnp.einsum(
            "nrs,nsv->nrv", transfer, jnp.repeat(downward, 2, axis=0), precision=PRECISE
        )
    nearby = jnp.einsum("npq,nqv->npv", blocks, current, precision=PRECISE)
    return nearby + jnp.einsum("npr,nrv->npv", basis_rows, downward, precision=PRECISE)


def spread(part, axis):
    size = lax.axis_size(axis)
    copies = jnp.broadcast_to(part[None], (size,) + part.shape)
    return lax.all_to_all(copies, axis, 0, 0, tiled=True)


def reduce_all(share):
    lower = lax.axis_size("lo")
    pieces = share.reshape(lower, share.shape[0] // lower, share.shape[1])
    piece = jnp.sum(lax.all_to_all(pieces, "lo", 0, 0, tiled=True), axis=0)
    piece = jnp.sum(spread(piece, "hi"), axis=0)
    return spread(piece, "lo").reshape(share.shape)


def body(
    embeddings,
    leaf_order,
    vectors_now,
    vectors_prior,
    leaf_bases,
    low_transfer,
    low_couple,
    middle_transfer,
    middle_couple,
    top_transfer,
    top_couple,
):
    leaf_count, leaf_size = leaf_order.shape
    points = embeddings.reshape(leaf_count, leaf_size, embeddings.shape[-1])
    inner_products = jnp.einsum(
        "npe,nqe->npq", points, points, preferred_element_type=jnp.float32
    )
    squares = jnp.diagonal(inner_products, axis1=1, axis2=2)
    distance = squares[:, :, None] + squares[:, None, :] - 2.0 * inner_products
    blocks = jnp.exp(-distance / (KERNEL_WIDTH * embeddings.shape[1]))
    chosen = (
        jnp.arange(leaf_size, dtype=jnp.int32)[None, :, None] == leaf_order[:, None, :]
    ).astype(jnp.float32)
    basis_rows = jnp.einsum(
        "nip,npr->nir",
        chosen,
        leaf_bases.reshape(leaf_count, leaf_size, leaf_bases.shape[-1]),
        precision=PRECISE,
    )
    tables = (low_transfer, low_couple, middle_transfer, middle_couple, top_transfer, top_couple)
    previous = vectors_prior.reshape(leaf_count, leaf_size, -1)
    current = vectors_now.reshape(leaf_count, leaf_size, -1)
    for degree_index in range(DEGREE):
        applied = apply_kernel(current, blocks, basis_rows, tables)
        previous, current = (
            current,
            2.0 / FILTER_HALF * (applied - FILTER_CENTER * current) - previous,
        )
    flattened = current.reshape(-1, current.shape[-1])
    points_total = flattened.shape[0] * lax.axis_size("hi") * lax.axis_size("lo")
    gram_total = (
        reduce_all(jnp.dot(flattened.T, flattened, precision=PRECISE)) / points_total
    )
    filtered = flattened
    filtered_prior = previous.reshape(flattened.shape)
    return (filtered, filtered_prior, gram_total)


def solution(mesh):
    placed = (
        P(("hi", "lo"), None),
        P(("hi", "lo"), None),
        P(("hi", "lo"), None),
        P(("hi", "lo"), None),
        P(("hi", "lo"), None),
        P(("hi", "lo"), None, None),
        P(("hi", "lo"), None, None),
        P("hi", None, None, None),
        P("hi", None, None, None),
        P(),
        P(),
    )
    return jax.shard_map(
        body,
        mesh=mesh,
        in_specs=placed,
        out_specs=(P(("hi", "lo"), None), P(("hi", "lo"), None), P()),
        check_vma=False,
    )
```

```python
import jax
import jax.numpy as jnp
from jax import lax
from jax.sharding import PartitionSpec as P

DEGREE = 6


KERNEL_WIDTH = 0.5
FILTER_CENTER = 2.0
FILTER_HALF = 10.0
PRECISE = lax.Precision.HIGHEST
STEP = 2.0 / FILTER_HALF


def ein(spec, *values):
    return jnp.einsum(spec, *values, precision=PRECISE)


def wide(values):
    return values.astype(jnp.float32)


def spread(part, axis):
    size = lax.axis_size(axis)
    copies = jnp.broadcast_to(part[None], (size,) + part.shape)
    return lax.all_to_all(copies, axis, 0, 0, tiled=True)


def reduce_all(share):
    lower = lax.axis_size("lo")
    pieces = share.reshape(lower, share.shape[0] // lower, share.shape[1])
    piece = jnp.sum(lax.all_to_all(pieces, "lo", 0, 0, tiled=True), axis=0)
    piece = jnp.sum(spread(piece, "hi"), axis=0)
    return spread(piece, "lo").reshape(share.shape)


def upper_matrices(top_transfer, top_couple):
    bits = lax.axis_size("hi").bit_length() - 1
    own = lax.axis_index("hi")
    rank = top_couple.shape[-1]
    sources = {}
    path = None
    for depth in range(bits, 0, -1):
        node = own >> (bits - depth)
        couple = wide(lax.dynamic_index_in_dim(top_couple, 2**depth - 2 + node, 0, keepdims=False))
        sources[depth] = couple.T if path is None else ein("rx,sx->rs", couple.T, path)
        if depth > 1:
            transfer = wide(
                lax.dynamic_index_in_dim(top_transfer, 2**depth - 4 + node, 0, keepdims=False)
            )
            path = transfer if path is None else ein("rs,sx->rx", path, transfer)
    reached = None
    for depth in range(1, bits + 1):
        number = 2**depth
        sibling = (own >> (bits - depth)) ^ 1
        if reached is None:
            carried = jnp.zeros((number, rank, rank), jnp.float32)
        else:
            transfer = wide(top_transfer[number - 4 : 2 * number - 4])
            carried = ein(
                "jirs,jsx->jirx", transfer.reshape(number // 2, 2, rank, rank), reached
            ).reshape(number, rank, rank)
        reached = jnp.where(
            jnp.arange(number)[:, None, None] == sibling, sources[depth][None], carried
        )
    return reached.reshape(-1, rank)


def group_matrices(transfer, couple, middle_transfer, middle_couple):
    nodes, rank = transfer.shape[0], transfer.shape[-1]
    bits = nodes.bit_length() - 1
    position = jnp.arange(nodes)
    near = (position[:, None] == (position ^ 1)[None, :])[:, None, :, None]
    mirrored = jnp.swapaxes(couple, 1, 2)
    total = jnp.where(near, jnp.swapaxes(mirrored, 0, 1)[None], 0.0)
    lift = transfer
    for depth in range(bits - 1, 0, -1):
        number = 2**depth
        share = nodes // number
        grouped = lift.reshape(number, share, rank, rank)
        image = ein(
            "ajsx,axy->ajsy", grouped, wide(middle_couple[number - 2 : 2 * number - 2])
        ).reshape(nodes * rank, rank)
        product = ein("ix,jx->ij", lift.reshape(nodes * rank, rank), image)
        level = position // share
        near = (level[:, None] == (level ^ 1)[None, :])[:, None, :, None]
        total = jnp.where(near, product.reshape(nodes, rank, nodes, rank), total)
        lift = ein(
            "ajsx,axy->ajsy", grouped, wide(middle_transfer[number - 2 : 2 * number - 2])
        ).reshape(nodes, rank, rank)
    return total.reshape(nodes * rank, nodes * rank), lift.reshape(nodes * rank, rank)


def body(
    embeddings,
    leaf_order,
    vectors_now,
    vectors_prior,
    leaf_bases,
    low_transfer,
    low_couple,
    middle_transfer,
    middle_couple,
    top_transfer,
    top_couple,
):
    leaf_count, leaf_size = leaf_order.shape
    rank = leaf_bases.shape[-1]
    vecs = vectors_now.shape[-1]
    lower = lax.axis_size("lo")
    upper = lax.axis_size("hi")
    piece = vecs // lower
    points_count = vectors_now.shape[0]
    device_tables = lax.all_gather(
        lax.optimization_barrier(jnp.stack((wide(low_transfer[0]), wide(low_couple[0])))), "lo"
    )
    points = embeddings.reshape(leaf_count, leaf_size, embeddings.shape[-1])
    inner_products = jnp.einsum(
        "npe,nqe->npq", points, points, preferred_element_type=jnp.float32
    )
    squares = jnp.diagonal(inner_products, axis1=1, axis2=2)
    distance = squares[:, :, None] + squares[:, None, :] - 2.0 * inner_products
    blocks = jnp.exp(-distance / (KERNEL_WIDTH * embeddings.shape[1]))
    chosen = (
        jnp.arange(leaf_size, dtype=jnp.int32)[None, :, None] == leaf_order[:, None, :]
    ).astype(jnp.float32)
    basis_rows = ein("nip,npr->nir", chosen, leaf_bases.reshape(leaf_count, leaf_size, rank))
    coupled_rows = ein("nir,nrs->nis", basis_rows, wide(low_couple[1:3]))
    cross = ein("nis,njs->nij", coupled_rows, basis_rows[::-1])
    local = jnp.concatenate(
        (
            jnp.concatenate((blocks[0], cross[0]), axis=1),
            jnp.concatenate((cross[1], blocks[1]), axis=1),
        ),
        axis=0,
    )
    local = STEP * (local - FILTER_CENTER * jnp.eye(points_count, dtype=jnp.float32))
    basis = ein("nir,nrs->nis", basis_rows, wide(low_transfer[1:3])).reshape(points_count, rank)

    states = [jnp.concatenate((vectors_now, basis), axis=1)]
    older = jnp.concatenate((vectors_prior, jnp.zeros_like(basis)), axis=1)
    for _ in range(DEGREE):
        following = jnp.dot(local, states[-1], precision=PRECISE) - older
        older = states[-1]
        states.append(following)
    projected = [ein("pc,pr->cr", states[k], basis) for k in range(DEGREE)]
    first_moment = lax.all_gather(projected[0][vecs:], "lo")
    later_moments = lax.all_gather(
        jnp.stack([projected[k][vecs:] for k in range(1, DEGREE - 1)]), "lo"
    )
    moments = [first_moment] + [later_moments[:, k] for k in range(DEGREE - 2)]
    outgoing = jnp.stack(
        [projected[k][:vecs].reshape(lower, piece, rank) for k in range(DEGREE)], axis=1
    )
    own_part = lax.all_to_all(outgoing, "lo", 0, 0, tiled=True)

    far = upper_matrices(top_transfer, top_couple)
    inside, lift = group_matrices(
        device_tables[:, 0], device_tables[:, 1], middle_transfer[0], middle_couple[0]
    )
    forward = jnp.concatenate((inside, lift), axis=1)

    images = []
    for k in range(DEGREE):
        coeffs = own_part[:, k]
        for j in range(k):
            coeffs = coeffs + STEP * ein("lcr,lrs->lcs", images[j], moments[k - 1 - j])
        flat = coeffs.transpose(1, 0, 2).reshape(piece, lower * rank)
        result = jnp.dot(flat, forward, precision=PRECISE)
        gathered = spread(result[:, lower * rank :], "hi")
        gathered = gathered.transpose(1, 0, 2).reshape(piece, upper * rank)
        reached = jnp.dot(gathered, far, precision=PRECISE)
        image = result[:, : lower * rank] + ein("cr,sr->cs", reached, lift)
        images.append(image.reshape(piece, lower, rank).transpose(1, 0, 2))

    returned = lax.all_to_all(jnp.stack(images, axis=1), "lo", 0, 0, tiled=True)
    returned = returned.transpose(0, 2, 1, 3).reshape(vecs, DEGREE * rank)
    responses = jnp.concatenate([states[DEGREE - 1 - j][:, vecs:] for j in range(DEGREE)], axis=1)
    filtered = states[DEGREE][:, :vecs] + STEP * ein("pk,ck->pc", responses, returned)
    filtered_prior = states[DEGREE - 1][:, :vecs] + STEP * ein(
        "pk,ck->pc", responses[:, rank:], returned[:, : (DEGREE - 1) * rank]
    )
    points_total = points_count * upper * lower
    gram_total = reduce_all(ein("pc,pd->cd", filtered, filtered)) / points_total
    return (filtered, filtered_prior, gram_total)


def solution(mesh):
    placed = (
        P(("hi", "lo"), None),
        P(("hi", "lo"), None),
        P(("hi", "lo"), None),
        P(("hi", "lo"), None),
        P(("hi", "lo"), None),
        P(("hi", "lo"), None, None),
        P(("hi", "lo"), None, None),
        P("hi", None, None, None),
        P("hi", None, None, None),
        P(),
        P(),
    )
    return jax.shard_map(
        body,
        mesh=mesh,
        in_specs=placed,
        out_specs=(P(("hi", "lo"), None), P(("hi", "lo"), None), P()),
        check_vma=False,
    )
```
